128 devices in a mesh: row: 16 (over y, z), col: 8 (over x, core).
Axes of the slice: x: 4, y: 4, z: 4, core: 2. Of those that a mesh axis runs over, the one named last changes fastest.
Arguments:
- right_side: bfloat16 [8, 16, 8, 128, 512], P(None, 'row', 'col'), may hold values from -6 to 6
- diag_inverse: bfloat16 [8, 16, 8, 128, 128], P(None, 'row', 'col'), may hold values from -1.5 to 1.5, as said below
- factor: bfloat16 [7, 16, 16, 8, 4, 128, 128], P(None, None, 'row', 'col'), may hold values from -0.0625 to 0.0625
- sources: int32 [7, 16, 16, 8, 4], P(None, None, 'row', 'col'), may hold values from 0 to 55, as said below
Outputs:
- solution: float32 [8, 16, 8, 128, 512], P(None, 'row', 'col')
The draws below stay inside these ranges and needn't reach their ends.
Inputs may be any that keep to these rules, and one draw needn't show every extreme that they name: `diag_inverse`: each block is the inverse of a lower triangular diagonal block of the factor, hence lower triangular. `sources`: for a target of level l (first index l - 1), each entry numbers a solved block of a level below l in the same source grid row r as level * 8 + grid column. The 4 entries of one target, source grid row and target grid column are distinct; the first 2 lie in level l - 1 and the last 2 in levels below l - 1, except for l = 1, where all lie in level 0.
All inputs are finite; a program needn't handle non-finite values.
Results may differ from the reference program's by a relative error of at most 0.008.
Values may be sent and summed in bfloat16 or wider, within the bound.
No kernel may reach another device: no remote copies, remote signals or barrier semaphores. Data moves between devices by JAX's collectives and lax.ppermute only.
A program may use at most 192 MiB of HBM per device.

```python
import math
import jax
import jax.numpy as jnp
from jax import lax

BS = 128
NRHS = 512
LEVELS = 8
KN = 2
KO = 2
KS = 4
N_ROW = 16
N_COL = 8


def draw_diag_inverse(key, part):
    first_key, second_key = jax.random.split(jax.random.fold_in(key, 11))
    shape = (LEVELS, N_ROW, N_COL, BS, BS)
    row_pos = lax.broadcasted_iota(jnp.int32, shape, 3)
    col_pos = lax.broadcasted_iota(jnp.int32, shape, 4)
    lower = jax.random.truncated_normal(first_key, -3.0, 3.0, shape, jnp.float32) * (0.5 / math.sqrt(BS))
    diagonal = jax.random.uniform(second_key, shape, jnp.float32, 0.6, 1.4)
    zeros_full = jnp.zeros(shape, jnp.float32)
    result = jnp.where(row_pos > col_pos, lower, jnp.where(row_pos == col_pos, diagonal, zeros_full))
    return result.astype(jnp.bfloat16)


def pick_distinct(key, pool_size, how_many, boosted):
    grid = (N_ROW, N_ROW, N_COL, pool_size)
    position = lax.broadcasted_iota(jnp.int32, grid, 3)
    corner = (lax.broadcasted_iota(jnp.int32, grid, 0) == 0) & (lax.broadcasted_iota(jnp.int32, grid, 1) == 0) & (lax.broadcasted_iota(jnp.int32, grid, 2) == 0)
    scores = jax.random.randint(key, grid, 0, 1 << 16, jnp.int32) * pool_size + position
    chosen = jnp.zeros(grid, jnp.bool_)
    for target in boosted:
        chosen = chosen | (position == target)
    scores = scores + jnp.where(corner & chosen, 1 << 28, 0).astype(jnp.int32)
    unused, picked = lax.top_k(scores, how_many)
    return picked.astype(jnp.int32)


def draw_sources(key, part):
    collected = []
    for level_index in range(1, LEVELS):
        level_key = jax.random.fold_in(jax.random.fold_in(key, 23), level_index)
        recent_key, older_key = jax.random.split(level_key)
        if level_index == 1:
            picked = pick_distinct(recent_key, N_COL, KS, (0, N_COL - 1))
        else:
            recent = pick_distinct(recent_key, N_COL, KN, (N_COL - 1,)) + (level_index - 1) * N_COL
            older = pick_distinct(older_key, (level_index - 1) * N_COL, KO, (0,))
            picked = jnp.concatenate([recent, older], axis=-1)
        collected.append(picked)
    return jnp.stack(collected).astype(jnp.int32)


def raised(values, own_key, source, target, shards_of, factor):
    owner, partner = [(jnp.arange(values.shape[dim]) // (values.shape[dim] // shards_of)).reshape([-1 if axis == dim else 1 for axis in range(values.ndim)]) for dim in (source, target)]
    chosen = jax.random.permutation(own_key, shards_of)[partner]
    strong = (owner == chosen) | (owner == (partner + shards_of // 2) % shards_of)
    return jnp.where(strong, factor * values, values)


def block_scale(own_key, extent, cuts, least, largest):
    factor_of = 1.0
    for dim, blocks in cuts:
        steps = jax.random.uniform(jax.random.fold_in(jax.random.fold_in(own_key, 6), dim), (blocks,), jnp.float32, least / len(cuts), largest / len(cuts))
        factor_of = factor_of * jnp.repeat(jnp.exp(steps), extent[dim] // blocks).reshape((-1,) + (1,) * (len(extent) - 1 - dim))
    return factor_of


def gaussian(own_key, dims, scale, reach, cuts=(), kind=jnp.bfloat16):
    level = block_scale(own_key, dims, cuts, -0.22, 0.18) if cuts else 1.0
    array = jax.random.normal(own_key, dims, jnp.float32) * scale * level
    return jnp.minimum(jnp.maximum(array, -reach), reach).astype(kind)


def bell_draw_with(key, extent, width, most, cuts, heavy, kind=jnp.bfloat16):
    entries = width * jax.random.normal(key, extent, jnp.float32)
    if cuts:
        entries = entries * block_scale(key, extent, cuts, -0.22, 0.18)
    return jnp.clip(raised(entries, jax.random.fold_in(key, 3), *heavy), -most, most).astype(kind)


def setup_inputs(seed: int = 0) -> dict:
    key_list = jax.random.split(jax.random.key(seed), 5)
    return {
        "right_side": gaussian(key_list[0], (LEVELS, N_ROW, N_COL, BS, NRHS), 1.0, 6.0, ((1, 16), (2, 8))),
        "diag_inverse": draw_diag_inverse(jax.random.fold_in(key_list[4], 71), 0),
        "factor": bell_draw_with(key_list[2], (LEVELS - 1, N_ROW, N_ROW, N_COL, KS, BS, BS), (2 * BS * KS * N_ROW) ** -0.5, 0.0625, ((2, 16), (3, 8)), (2, 1, 16, 2.0)),
        "sources": draw_sources(jax.random.fold_in(key_list[4], 71), 0),
    }


def reference(right_side, diag_inverse, factor, sources):
    solved_list = []
    solution_list = []
    for level_index in range(LEVELS):
        if level_index == 0:
            reduced = right_side[0]
        else:
            history = jnp.stack(solved_list, axis=1).reshape(N_ROW, level_index * N_COL, BS, NRHS)
            grid_rows = jnp.arange(N_ROW, dtype=jnp.int32)[:, None, None]

            def target_row(operands):
                blocks, source_ids = operands
                picked = history[grid_rows, source_ids.astype(jnp.int32)]
                partial_value = jnp.einsum("rckab,rckbn->rcan", blocks.astype(jnp.float32), picked.astype(jnp.float32))
                return jnp.sum(partial_value, axis=0)

            update = lax.map(target_row, (factor[level_index - 1], sources[level_index - 1]))
            reduced = (right_side[level_index].astype(jnp.float32) - update).astype(jnp.bfloat16)
        solution = jnp.einsum("pqab,pqbn->pqan", diag_inverse[level_index].astype(jnp.float32), reduced.astype(jnp.float32))
        solution_list.append(solution)
        solved_list.append(solution.astype(jnp.bfloat16))
    return jnp.stack(solution_list)
```

```python
import functools

import jax
import jax.numpy as jnp
from jax import lax
from jax.experimental import pallas as pl
from jax.experimental.pallas import tpu as pltpu
from jax.sharding import PartitionSpec as P


BF16 = jnp.bfloat16
F32 = jnp.float32
SIDE = 4
AXES = ("row", "col")
VMEM = pl.BlockSpec(memory_space=pltpu.VMEM)
SMEM = pl.BlockSpec(memory_space=pltpu.SMEM)


def device_pairs(move):
    pairs = []
    for y in range(SIDE):
        for z in range(SIDE):
            for x in range(SIDE):
                for core in range(2):
                    ty, tz, tx, tc = move(y, z, x, core)
                    source = ((y * SIDE + z) * SIDE + x) * 2 + core
                    target = ((ty % SIDE * SIDE + tz % SIDE) * SIDE + tx % SIDE) * 2 + tc
                    pairs.append((source, target))
    return pairs


def first_axis(shift):
    return device_pairs(lambda y, z, x, c: (y, z + shift, x, c) if c == 0 else (y + shift, z, x, c))


def second_axis(shift):
    return device_pairs(lambda y, z, x, c: (y + shift, z, x, c) if c == 0 else (y, z + shift, x, c))


def along_x(shift):
    return device_pairs(lambda y, z, x, c: (y, z, x + shift, c))


SWAP_CORES = device_pairs(lambda y, z, x, c: (y, z, x, 1 - c))


def send(value, pairs):
    return lax.ppermute(value, AXES, pairs)


def place():
    row = lax.axis_index("row")
    core = lax.axis_index("col") % 2
    y, z = row // SIDE, row % SIDE
    return core, jnp.where(core == 0, z, y), jnp.where(core == 0, y, z)


def target_row(core, first, shift, j):
    there = (first + shift) % SIDE
    return jnp.where(core == 0, j * SIDE + there, there * SIDE + j)


def older_kernel(level, ids, where, factor, *refs):
    parts, (out, pool, sems) = refs[:-3], refs[-3:]
    copies = [
        pltpu.make_async_copy(part, pool.at[pl.ds(4 * i, 4)], sems.at[i])
        for i, part in enumerate(parts)
    ]
    for copy in copies:
        copy.start()
    for copy in copies:
        copy.wait()

    def step(t, carry):
        p = where[t]
        base = ((level - 1) * 16 + p) * 4
        left = jnp.concatenate([factor[0, p, 0], factor[0, p, 1]], axis=1)
        right = jnp.concatenate([pool[ids[base + 2]], pool[ids[base + 3]]], axis=0)
        out[t] = jnp.dot(left, right, preferred_element_type=F32)
        return carry

    lax.fori_loop(0, 16, step, 0, unroll=2)


def recent_kernel(level, slots, ids, where, factor, mine, swapped, *refs):
    older = refs[0] if level > 1 else None
    keep, out1, out2, out3, pool = refs[-5:]
    pool[0:4] = mine[...]
    pool[4:8] = swapped[...]
    for shift, out in ((2, out2), (1, out1), (3, out3), (0, keep)):
        for j in range(SIDE):
            t = shift * SIDE + j
            p = where[t]
            base = ((level - 1) * 16 + p) * 4
            left = jnp.concatenate([factor[0, p, k] for k in range(slots)], axis=1)
            right = jnp.concatenate([pool[ids[base + k]] for k in range(slots)], axis=0)
            value = jnp.dot(left, right, preferred_element_type=F32)
            if older is not None:
                value = value + older[t]
            out[j] = value.astype(out.dtype)


def sum_kernel(where, keep, got1, got2, got3, own, out1, out2, out3):
    second = where[16]
    for shift, out in ((2, out2), (1, out1), (3, out3), (0, own)):
        j = (second + shift) % SIDE
        value = keep[j] + got1[j].astype(F32) + got2[j].astype(F32) + got3[j].astype(F32)
        out[...] = value.astype(out.dtype)


def solve_kernel(side, inverse, *refs):
    *updates, solution, solved = refs
    reduced = side[0, 0, 0]
    if updates:
        total = updates[0][...]
        for update in updates[1:]:
            total = total + update[...].astype(F32)
        reduced = (reduced.astype(F32) - total).astype(BF16)
    value = jnp.dot(inverse[0, 0, 0], reduced, preferred_element_type=F32)
    solution[...] = value
    solved[...] = value.astype(BF16)


def shaped(shape, dtype):
    return jax.ShapeDtypeStruct(shape, dtype)


def limit(mib):
    return pltpu.CompilerParams(vmem_limit_bytes=mib * 2**20)


def cost(flops, nbytes):
    return pl.CostEstimate(flops=flops, bytes_accessed=nbytes, transcendentals=0)


def per_device(right_side, diag_inverse, factor, sources):
    levels, bs, nrhs = right_side.shape[0], right_side.shape[3], right_side.shape[4]
    core, first, second = place()
    x = lax.axis_index("col") // 2
    source_col = sources % 8
    relative = ((source_col % 2) ^ core) * SIDE + (source_col // 2 - x) % SIDE
    older_ids = (sources // 8) * 8 + relative
    slot = lax.broadcasted_iota(jnp.int32, sources.shape, 4)
    ids = jnp.where((slot < 2) | (lax.broadcasted_iota(jnp.int32, sources.shape, 0) == 0), relative, older_ids)
    ids = ids.reshape(-1)
    t = jnp.arange(17, dtype=jnp.int32)
    where = jnp.where(t < 16, target_row(core, first, t // SIDE, t % SIDE), second)
    factor = factor.reshape(factor.shape[0], 16, 4, bs, bs)
    block = shaped((bs, nrhs), BF16)
    message = shaped((SIDE, bs, nrhs), BF16)

    def solve(level, updates):
        return pl.pallas_call(
            solve_kernel,
            grid=(1,),
            in_specs=[
                pl.BlockSpec((1, 1, 1, bs, nrhs), lambda i: (level, 0, 0, 0, 0)),
                pl.BlockSpec((1, 1, 1, bs, bs), lambda i: (level, 0, 0, 0, 0)),
            ]
            + [VMEM] * len(updates),
            out_specs=[VMEM, VMEM],
            out_shape=[shaped((bs, nrhs), F32), block],
            name="solve",
            compiler_params=limit(4),
            cost_estimate=cost(2 * bs * bs * nrhs, 2**20),
        )(right_side, diag_inverse, *updates)

    def gather(solved):
        got = [send(solved, along_x(-d)) for d in (1, 2, 3)]
        mine = jnp.stack([solved, *got])
        return mine, send(mine, SWAP_CORES)

    def products_with_older(level, parts):
        return pl.pallas_call(
            functools.partial(older_kernel, level),
            grid=(1,),
            in_specs=[SMEM, SMEM, pl.BlockSpec((1, 16, 2, bs, bs), lambda i: (level - 1, 0, 1, 0, 0))]
            + [pl.BlockSpec(memory_space=pl.ANY)] * len(parts),
            out_specs=VMEM,
            out_shape=shaped((16, bs, nrhs), F32),
            scratch_shapes=[
                pltpu.VMEM((4 * len(parts), bs, nrhs), BF16),
                pltpu.SemaphoreType.DMA((len(parts),)),
            ],
            name="older",
            compiler_params=limit(20),
            cost_estimate=cost(2**30 // 2, 2**23),
        )(ids, where, factor, *parts)

    def messages(level, mine, swapped, older):
        slots = 4 if level == 1 else 2
        return pl.pallas_call(
            functools.partial(recent_kernel, level, slots),
            grid=(1,),
            in_specs=[SMEM, SMEM, pl.BlockSpec((1, 16, slots, bs, bs), lambda i: (level - 1, 0, 0, 0, 0)), VMEM, VMEM]
            + [VMEM] * len(older),
            out_specs=[VMEM] * 4,
            out_shape=[shaped(message.shape, F32), message, message, message],
            scratch_shapes=[pltpu.VMEM((8, bs, nrhs), BF16)],
            name="recent",
            compiler_params=limit(20),
            cost_estimate=cost(2**30 // 2, 2**23),
        )(ids, where, factor, mine, swapped, *older)

    def sums(keep, got):
        return pl.pallas_call(
            sum_kernel,
            in_specs=[SMEM] + [VMEM] * 4,
            out_specs=[VMEM] * 4,
            out_shape=[shaped((bs, nrhs), F32), block, block, block],
            name="sums",
            compiler_params=limit(8),
            cost_estimate=cost(2**22, 2**22),
        )(where, keep, *got)

    solution, solved = solve(0, [])
    solutions = [solution]
    parts = []
    mine, swapped = gather(solved)
    for level in range(1, levels):
        older = [products_with_older(level, parts)] if level > 1 else []
        keep, *out = messages(level, mine, swapped, older)
        parts = [*parts, mine, swapped]
        got = [send(out[d - 1], first_axis(d)) for d in (1, 2, 3)]
        own, *out = sums(keep, got)
        got = [send(out[d - 1], second_axis(d)) for d in (1, 2, 3)]
        solution, solved = solve(level, [own, *got])
        solutions.append(solution)
        if level + 1 < levels:
            mine, swapped = gather(solved)
    return jnp.stack(solutions)[:, None, None]


def solution(mesh):
    placed = (
        P(None, "row", "col", None, None),
        P(None, "row", "col", None, None),
        P(None, None, "row", "col", None, None, None),
        P(None, None, "row", "col", None),
    )
    return jax.shard_map(
        per_device,
        mesh=mesh,
        in_specs=placed,
        out_specs=P(None, "row", "col", None, None),
        check_vma=False,
    )
```

```python
import functools

import jax
import jax.numpy as jnp
from jax import lax
from jax.experimental import pallas as pl
from jax.experimental.pallas import tpu as pltpu
from jax.sharding import PartitionSpec as P


BF16 = jnp.bfloat16
F32 = jnp.float32
SIDE = 4
AXES = ("row", "col")
AHEAD_LIMIT = 36
VMEM = pl.BlockSpec(memory_space=pltpu.VMEM)
ANY = pl.BlockSpec(memory_space=pl.ANY)
SMEM = pl.BlockSpec(memory_space=pltpu.SMEM)


def device_pairs(move):
    pairs = []
    for y in range(SIDE):
        for z in range(SIDE):
            for x in range(SIDE):
                for core in range(2):
                    ty, tz, tx, tc = move(y, z, x, core)
                    source = ((y * SIDE + z) * SIDE + x) * 2 + core
                    target = ((ty % SIDE * SIDE + tz % SIDE) * SIDE + tx % SIDE) * 2 + tc
                    pairs.append((source, target))
    return pairs


def first_axis(shift):
    return device_pairs(lambda y, z, x, c: (y, z + shift, x, c) if c == 0 else (y + shift, z, x, c))


def second_axis(shift):
    return device_pairs(lambda y, z, x, c: (y + shift, z, x, c) if c == 0 else (y, z + shift, x, c))


def along_x(shift):
    return device_pairs(lambda y, z, x, c: (y, z, x + shift, c))


SWAP_CORES = device_pairs(lambda y, z, x, c: (y, z, x, 1 - c))


def send(value, pairs):
    return lax.ppermute(value, AXES, pairs)


def place():
    row = lax.axis_index("row")
    core = lax.axis_index("col") % 2
    y, z = row // SIDE, row % SIDE
    return core, jnp.where(core == 0, z, y), jnp.where(core == 0, y, z)


def target_row(core, first, shift, j):
    there = (first + shift) % SIDE
    return jnp.where(core == 0, j * SIDE + there, there * SIDE + j)


def run_copies(pairs, sems):
    copies = [pltpu.make_async_copy(a, b, sems.at[i]) for i, (a, b) in enumerate(pairs)]
    for copy in copies:
        copy.start()
    for copy in copies:
        copy.wait()


def ahead_kernel(level, ids, where, factor, side, inverse, *refs):
    count = 2 * (level - 1)
    parts, refs = refs[:count], refs[count:]
    side_out, inverse_out, blocks, *refs, sems = refs
    slots = blocks.shape[1]
    pairs = [
        (factor.at[level - 1, :, 0, 0, pl.ds(0, slots)], blocks),
        (side.at[level, 0, 0], side_out),
        (inverse.at[level, 0, 0], inverse_out),
    ]
    if count:
        total, pool, older = refs
        pairs += [(factor.at[level - 1, :, 0, 0, pl.ds(2, 2)], older)]
        pairs += [(part, pool.at[pl.ds(4 * i, 4)]) for i, part in enumerate(parts)]
    run_copies(pairs, sems)
    if not count:
        return

    def step(t, carry):
        p = where[t]
        base = ((level - 1) * 16 + p) * 4
        left = jnp.concatenate([older[p, 0], older[p, 1]], axis=1)
        right = jnp.concatenate([pool[ids[base + 2]], pool[ids[base + 3]]], axis=0)
        total[t] = jnp.dot(left, right, preferred_element_type=F32)
        return carry

    lax.fori_loop(0, 16, step, 0, unroll=2)


def recent_kernel(level, slots, ids, where, factor, mine, swapped, *refs):
    older = refs[0] if level > 1 else None
    keep, out1, out2, out3, pool = refs[-5:]
    pool[0:4] = mine[...]
    pool[4:8] = swapped[...]
    for shift, out in ((2, out2), (1, out1), (3, out3), (0, keep)):
        for j in range(SIDE):
            t = shift * SIDE + j
            p = where[t]
            base = ((level - 1) * 16 + p) * 4
            left = jnp.concatenate([factor[p, k] for k in range(slots)], axis=1)
            right = jnp.concatenate([pool[ids[base + k]] for k in range(slots)], axis=0)
            value = jnp.dot(left, right, preferred_element_type=F32)
            if older is not None:
                value = value + older[t]
            out[j] = value.astype(out.dtype)


def sum_kernel(where, keep, got1, got2, got3, own, out1, out2, out3):
    second = where[16]
    for shift, out in ((2, out2), (1, out1), (3, out3), (0, own)):
        j = (second + shift) % SIDE
        value = keep[j] + got1[j].astype(F32) + got2[j].astype(F32) + got3[j].astype(F32)
        out[...] = value.astype(out.dtype)


def solved_of(side, inverse, updates):
    reduced = side
    if updates:
        total = updates[0][...]
        for update in updates[1:]:
            total = total + update[...].astype(F32)
        reduced = (reduced.astype(F32) - total).astype(BF16)
    return jnp.dot(inverse, reduced, preferred_element_type=F32)


def first_solve_kernel(side, inverse, solution, solved, side_buf, inverse_buf, sems):
    run_copies([(side.at[0, 0, 0], side_buf), (inverse.at[0, 0, 0], inverse_buf)], sems)
    value = solved_of(side_buf[...], inverse_buf[...], [])
    solution[...] = value
    solved[...] = value.astype(BF16)


def solve_kernel(side, inverse, *refs):
    *updates, solution, solved = refs
    value = solved_of(side[...], inverse[...], updates)
    solution[...] = value
    solved[...] = value.astype(BF16)


def last_solve_kernel(side, inverse, *refs):
    *updates, whole, out = refs
    out[0] = solved_of(side[...], inverse[...], updates)


def assemble_kernel(*refs):
    *pieces, out = refs
    for i, piece in enumerate(pieces):
        out[i] = piece[...]


def shaped(shape, dtype):
    return jax.ShapeDtypeStruct(shape, dtype)


def limit(mib):
    return pltpu.CompilerParams(vmem_limit_bytes=mib * 2**20)


def cost(flops, nbytes):
    return pl.CostEstimate(flops=flops, bytes_accessed=nbytes, transcendentals=0)


def per_device(right_side, diag_inverse, factor, sources):
    levels, bs, nrhs = right_side.shape[0], right_side.shape[3], right_side.shape[4]
    core, first, second = place()
    x = lax.axis_index("col") // 2
    source_col = sources % 8
    relative = ((source_col % 2) ^ core) * SIDE + (source_col // 2 - x) % SIDE
    older_ids = (sources // 8) * 8 + relative
    slot = lax.broadcasted_iota(jnp.int32, sources.shape, 4)
    ids = jnp.where((slot < 2) | (lax.broadcasted_iota(jnp.int32, sources.shape, 0) == 0), relative, older_ids)
    ids = ids.reshape(-1)
    t = jnp.arange(17, dtype=jnp.int32)
    where = jnp.where(t < 16, target_row(core, first, t // SIDE, t % SIDE), second)
    block = shaped((bs, nrhs), BF16)
    message = shaped((SIDE, bs, nrhs), BF16)

    def first_solve():
        return pl.pallas_call(
            first_solve_kernel,
            in_specs=[ANY, ANY],
            out_specs=[VMEM, VMEM],
            out_shape=[shaped((bs, nrhs), F32), block],
            scratch_shapes=[pltpu.VMEM((bs, nrhs), BF16), pltpu.VMEM((bs, bs), BF16), pltpu.SemaphoreType.DMA((2,))],
            name="first_solve",
            compiler_params=limit(62),
            cost_estimate=cost(2 * bs * bs * nrhs, 2**20),
        )(right_side, diag_inverse)

    def solve(side, inverse, updates):
        return pl.pallas_call(
            solve_kernel,
            in_specs=[VMEM] * (2 + len(updates)),
            out_specs=[VMEM, VMEM],
            out_shape=[shaped((bs, nrhs), F32), block],
            name="solve",
            compiler_params=limit(4),
            cost_estimate=cost(2 * bs * bs * nrhs, 2**20),
        )(side, inverse, *updates)

    def last_solve(side, inverse, updates, whole):
        return pl.pallas_call(
            last_solve_kernel,
            grid=(1,),
            in_specs=[VMEM] * (2 + len(updates)) + [ANY],
            out_specs=pl.BlockSpec((1, bs, nrhs), lambda i: (levels - 1, 0, 0)),
            out_shape=shaped((levels, bs, nrhs), F32),
            input_output_aliases={2 + len(updates): 0},
            name="last_solve",
            compiler_params=limit(4),
            cost_estimate=cost(2 * bs * bs * nrhs, 2**20),
        )(side, inverse, *updates, whole)

    def assemble(pieces):
        return pl.pallas_call(
            assemble_kernel,
            grid=(1,),
            in_specs=[VMEM] * len(pieces),
            out_specs=pl.BlockSpec((levels - 1, bs, nrhs), lambda i: (0, 0, 0)),
            out_shape=shaped((levels, bs, nrhs), F32),
            name="assemble",
            compiler_params=limit(16),
            cost_estimate=cost(0, 2**22),
        )(*pieces)

    def gather(solved):
        got = [send(solved, along_x(-d)) for d in (1, 2, 3)]
        mine = jnp.stack([solved, *got])
        return mine, send(mine, SWAP_CORES)

    def ahead(level, parts):
        slots = 2 if parts else 4
        out_shape = [block, shaped((bs, bs), BF16), shaped((16, slots, bs, bs), BF16)]
        scratch = []
        if parts:
            out_shape += [shaped((16, bs, nrhs), F32)]
            scratch = [pltpu.VMEM((4 * len(parts), bs, nrhs), BF16), pltpu.VMEM((16, 2, bs, bs), BF16)]
        return pl.pallas_call(
            functools.partial(ahead_kernel, level),
            in_specs=[SMEM, SMEM] + [ANY] * (3 + len(parts)),
            out_specs=[VMEM] * len(out_shape),
            out_shape=out_shape,
            scratch_shapes=[*scratch, pltpu.SemaphoreType.DMA((4 + len(parts),))],
            name="ahead",
            compiler_params=limit(AHEAD_LIMIT if parts else 48),
            cost_estimate=cost(2**29, 2**23),
        )(ids, where, factor, right_side, diag_inverse, *parts)

    def messages(level, blocks, mine, swapped, older):
        slots = 4 if level == 1 else 2
        return pl.pallas_call(
            functools.partial(recent_kernel, level, slots),
            in_specs=[SMEM, SMEM] + [VMEM] * (3 + len(older)),
            out_specs=[VMEM] * 4,
            out_shape=[shaped(message.shape, F32), message, message, message],
            scratch_shapes=[pltpu.VMEM((8, bs, nrhs), BF16)],
            name="recent",
            compiler_params=limit(20),
            cost_estimate=cost(2**30 // 2, 2**23),
        )(ids, where, blocks, mine, swapped, *older)

    def sums(keep, got):
        return pl.pallas_call(
            sum_kernel,
            in_specs=[SMEM] + [VMEM] * 4,
            out_specs=[VMEM] * 4,
            out_shape=[shaped((bs, nrhs), F32), block, block, block],
            name="sums",
            compiler_params=limit(8),
            cost_estimate=cost(2**22, 2**22),
        )(where, keep, *got)

    solutions, parts, older = [], [], []
    for level in range(levels):
        last = level + 1 == levels
        if level == 0:
            solution, solved = first_solve()
            mine, swapped = gather(solved)
            side, inverse, blocks = ahead(1, [])
            solutions.append(solution)
            continue
        keep, *out = messages(level, blocks, mine, swapped, older)
        got = [send(out[d - 1], first_axis(d)) for d in (1, 2, 3)]
        here = (side, inverse)
        if last:
            whole = assemble(solutions)
        else:
            parts = [*parts, mine, swapped]
            side, inverse, blocks, *older = ahead(level + 1, parts)
        own, *out = sums(keep, got)
        got = [send(out[d - 1], second_axis(d)) for d in (1, 2, 3)]
        if not last:
            solution, solved = solve(*here, [own, *got])
            solutions.append(solution)
            mine, swapped = gather(solved)
    result = last_solve(*here, [own, *got], whole)
    return result[:, None, None]


def solution(mesh):
    placed = (
        P(None, "row", "col", None, None),
        P(None, "row", "col", None, None),
        P(None, None, "row", "col", None, None, None),
        P(None, None, "row", "col", None),
    )
    return jax.shard_map(
        per_device,
        mesh=mesh,
        in_specs=placed,
        out_specs=P(None, "row", "col", None, None),
        check_vma=False,
    )
```
